32 devices in a mesh: grp: 8 (over y, x, core), head: 4 (over z).
Axes of the slice: x: 2, y: 2, z: 4, core: 2. Of those that a mesh axis runs over, the one named last changes fastest.
Arguments:
- q_nope: bfloat16 [4, 64, 128, 128], P(None, 'grp', 'head'), may hold values from -6 to 6
- q_rope: bfloat16 [4, 64, 128, 64], P(None, 'grp', 'head'), may hold values from -512 to 512
- w_absorb_k: bfloat16 [128, 128, 512], P('head'), may hold values from -0.5 to 0.5
- w_absorb_v: bfloat16 [128, 512, 128], P('head'), may hold values from -0.25 to 0.25
- latent_cache: bfloat16 [64, 1024, 576], P(('grp', 'head')), may hold values from -4 to 4
- new_latent: bfloat16 [4, 64, 576], P(None, ('grp', 'head')), may hold values from -6 to 6
- lengths: int32 [64], replicated, may hold values from 128 to 1020, as said below
- moves: int32 [4, 1], P('head'), may hold values from 1 to 7
Outputs:
- attended: bfloat16 [4, 64, 128, 128], P(None, 'grp', 'head')
The draws below stay inside these ranges and needn't reach their ends.
Inputs may be any that keep to these rules, and one draw needn't show every extreme that they name: lengths[r] counts the live rows of latent_cache[r]; its later rows up to 1024 are padding that no query reads.
All inputs are finite; a program needn't handle non-finite values.
Results may differ from the reference program's by a relative error of at most 0.0077.
Values may be sent and summed in bfloat16 or wider, within the bound.
A program may use at most 64 MiB of HBM per device.

```python
import math
import jax
import jax.numpy as jnp
from jax import lax

HEADS = 128
HEAD_DIM = 128
ROPE = 64
LATENT = 512
BLOCK = 128
STEPS = 4
REQ_DEV = 2
KV = 576
CAP = 1024
MOVERS = 1
GROUPS = 8
COLUMNS = 4
REQUESTS = 64


def first_keys(key):
    return jax.random.truncated_normal(jax.random.fold_in(key, 8), -4.0, 4.0, (REQUESTS, ROPE), jnp.float32)


def draw_latent_cache(key, part):
    shape = (REQUESTS, CAP, LATENT + ROPE)
    values = jax.random.truncated_normal(jax.random.fold_in(key, 7), -4.0, 4.0, shape, jnp.float32)
    values = values.at[:, 0, LATENT:].set(first_keys(key))
    return values.astype(jnp.bfloat16)


def draw_q_rope(key, part):
    shape = (STEPS, REQUESTS, HEADS, ROPE)
    values = jax.random.truncated_normal(jax.random.fold_in(key, 11), -4.0, 4.0, shape, jnp.float32)
    return values.astype(jnp.bfloat16)


def draw_lengths(key, part):
    spread_top = CAP - STEPS - BLOCK
    factor_one = jax.random.randint(jax.random.fold_in(key, 21), (REQUESTS,), 0, spread_top + 1)
    factor_two = jax.random.randint(jax.random.fold_in(key, 22), (REQUESTS,), 0, spread_top + 1)
    values = BLOCK + factor_one * factor_two // spread_top
    shuffled = jax.random.permutation(jax.random.fold_in(key, 23), REQUESTS)
    values = values.at[shuffled[0]].set(CAP - STEPS).at[shuffled[1]].set(BLOCK)
    return values.astype(jnp.int32)


def draw_moves(key, part):
    values = jax.random.randint(jax.random.fold_in(key, 31), (COLUMNS, MOVERS), 1, GROUPS)
    forced_at = jax.random.randint(jax.random.fold_in(key, 32), (), 0, COLUMNS * MOVERS)
    flattened = values.reshape(-1).at[forced_at].set(GROUPS - 1)
    return flattened.reshape(COLUMNS, MOVERS).astype(jnp.int32)


def block_scale(stream_key, dims, pieces, low, high):
    def one(dim, shards_of):
        draws = jax.random.uniform(jax.random.fold_in(jax.random.fold_in(stream_key, 6), dim), (shards_of,), jnp.float32, low / len(pieces), high / len(pieces))
        return jnp.repeat(jnp.exp(draws), dims[dim] // shards_of).reshape((-1,) + (1,) * (len(dims) - dim - 1))

    factor_of = one(*pieces[0])
    for cut in pieces[1:]:
        factor_of = factor_of * one(*cut)
    return factor_of


def normal_values(rng, dims, width, most, cuts=(), kind=jnp.bfloat16):
    result = width * jax.random.normal(rng, dims, jnp.float32)
    if cuts:
        result = result * block_scale(rng, dims, cuts, -0.22, 0.18)
    return jnp.clip(result, -most, most).astype(kind)


def setup_inputs(seed: int = 0) -> dict:
    splits = jax.random.split(jax.random.key(seed), 9)
    return {
        "q_nope": normal_values(splits[0], (STEPS, REQUESTS, HEADS, HEAD_DIM), 1.0, 6.0, ((1, 8), (2, 4))),
        "q_rope": draw_q_rope(jax.random.fold_in(splits[8], 71), 0),
        "w_absorb_k": normal_values(splits[2], (HEADS, HEAD_DIM, LATENT), HEAD_DIM ** -0.5, 0.5, ((0, 4),)),
        "w_absorb_v": normal_values(splits[3], (HEADS, LATENT, HEAD_DIM), LATENT ** -0.5, 0.25, ((0, 4),)),
        "latent_cache": draw_latent_cache(jax.random.fold_in(splits[8], 71), 0),
        "new_latent": normal_values(splits[5], (STEPS, REQUESTS, KV), 1.0, 6.0, ((1, 32),)),
        "lengths": draw_lengths(jax.random.fold_in(splits[8], 71), 0),
        "moves": draw_moves(jax.random.fold_in(splits[8], 71), 0),
    }


yarn_gain = (0.1 * math.log(40.0) + 1.0) ** 2

def home_slots(moves):
    group_ids = jnp.arange(GROUPS, dtype=jnp.int32)[:, None, None]
    column_ids = jnp.arange(COLUMNS, dtype=jnp.int32)[None, :, None]
    place_ids = jnp.arange(REQ_DEV, dtype=jnp.int32)[None, None, :]
    offsets = jnp.concatenate([moves.astype(jnp.int32), jnp.zeros((COLUMNS, REQ_DEV - MOVERS), jnp.int32)], axis=1)[None, :, :]
    source = jnp.mod(group_ids - offsets, GROUPS)
    return ((source * COLUMNS + column_ids) * REQ_DEV + place_ids).reshape(-1).astype(jnp.int32)

def attend_one(query_row, stored, live_count, recent, live_steps, score_scale):
    query_wide = query_row.astype(jnp.float32)
    scores = jnp.einsum('hc,tc->ht', query_wide, stored.astype(jnp.float32)) * score_scale
    positions = jnp.arange(stored.shape[0], dtype=jnp.int32)
    scores = jnp.where(positions[None, :] < live_count, scores, -jnp.inf)
    extra_scores = jnp.einsum('hc,jc->hj', query_wide, recent.astype(jnp.float32)) * score_scale
    extra_scores = jnp.where(live_steps[None, :], extra_scores, -jnp.inf)
    peak = jnp.maximum(lax.optimization_barrier(jnp.max(scores, axis=1)), lax.optimization_barrier(jnp.max(extra_scores, axis=1)))[:, None]
    spread = jnp.exp(scores - peak)
    spread_new = jnp.exp(extra_scores - peak)
    softmax_sum = lax.optimization_barrier(jnp.sum(spread, axis=1, keepdims=True)) + lax.optimization_barrier(jnp.sum(spread_new, axis=1, keepdims=True))
    weights = lax.optimization_barrier((spread / softmax_sum).astype(jnp.bfloat16)).astype(jnp.float32)
    weights_new = lax.optimization_barrier((spread_new / softmax_sum).astype(jnp.bfloat16)).astype(jnp.float32)
    mixed_rows = jnp.einsum('ht,tl->hl', weights, stored[:, :LATENT].astype(jnp.float32))
    mixed_rows = mixed_rows + jnp.einsum('hj,jl->hl', weights_new, recent[:, :LATENT].astype(jnp.float32))
    return mixed_rows.astype(jnp.bfloat16)

def reference(q_nope, q_rope, w_absorb_k, w_absorb_v, latent_cache, new_latent, lengths, moves):
    score_scale = yarn_gain / math.sqrt(HEAD_DIM + ROPE)
    own_rows = jnp.arange(REQUESTS, dtype=jnp.int32)
    moved_rows = home_slots(moves)
    batch_rows = COLUMNS * REQ_DEV
    step_ids = jnp.arange(STEPS, dtype=jnp.int32)
    results = []
    for moment in range(STEPS):
        home_rows = moved_rows if moment >= 2 else own_rows
        root = jnp.where(step_ids[None, :] < 2, home_rows[:, None], own_rows[:, None]).astype(jnp.int32)
        live_steps = step_ids <= moment
        q_latent = jnp.einsum('rhd,hdl->rhl', q_nope[moment].astype(jnp.float32), w_absorb_k.astype(jnp.float32)).astype(jnp.bfloat16)
        queries = jnp.concatenate([q_latent, q_rope[moment]], axis=2)

        def one_block(element):
            block_queries, block_home, block_root = element

            def one_request(query_row, source, chosen_rows):
                stored = lax.dynamic_index_in_dim(latent_cache, source, 0, keepdims=False)
                recent = new_latent[step_ids, chosen_rows]
                live_count = lengths[source]
                return attend_one(query_row, stored, live_count, recent, live_steps, score_scale)
            return jax.vmap(one_request)(block_queries, block_home, block_root)
        mixed_rows = lax.map(one_block, (queries.reshape(-1, batch_rows, HEADS, queries.shape[2]), home_rows.reshape(-1, batch_rows), root.reshape(-1, batch_rows, STEPS)))
        mixed_rows = mixed_rows.reshape(REQUESTS, HEADS, LATENT)
        results.append(jnp.einsum('rhl,hld->rhd', mixed_rows.astype(jnp.float32), w_absorb_v.astype(jnp.float32)).astype(jnp.bfloat16))
    return jnp.stack(results)
```

```python
import functools
import math

import jax
import jax.numpy as jnp
from jax import lax
from jax.experimental import pallas as pl
from jax.experimental.pallas import tpu as pltpu
from jax.sharding import PartitionSpec as P

PAIR = 2
EXTRA = 128
LANES = 128
YARN_GAIN = (0.1 * math.log(40.0) + 1.0) ** 2
MESH = pl.DeviceIdType.MESH


def lane(c):
    return slice(c * LANES, (c + 1) * LANES)


def rounded(value):
    return value.astype(jnp.bfloat16)


def wide(value):
    return value.astype(jnp.float32)


def kernel(
    groups, columns, scale,
    length_ref, move_ref, nope_ref, rope_ref, fresh_ref, wk_hbm, wv_hbm, cache_hbm,
    out_ref,
    wk, wv, keys, local_sem,
    rows_in, rows_mid, rows_out,
    lat_send, lat_recv, rot_send, rot_recv, back_send, back_recv,
    mine, moved, mine_key, moved_key, home, home_recv, shift_of, shift_mine,
    lat_ss, lat_rs, rot_ss, rot_rs, back_ss, back_rs,
    mine_ss, mine_rs, key_ss, key_rs, home_ss, home_rs, shift_ss, shift_rs,
):
    steps, _, heads, _ = nope_ref.shape
    holders, capacity, entries = cache_hbm.shape
    latent = wk.shape[2]
    rope = entries - latent
    movers = move_ref.shape[1]
    spans = steps // PAIR
    total = capacity + EXTRA
    rank = lax.axis_index("grp")
    column = lax.axis_index("head")
    parts = wk.shape[0] // local_part(heads)
    part = local_part(heads)

    wk_copies = [
        pltpu.make_async_copy(
            wk_hbm.at[pl.ds(n * part, part)], wk.at[pl.ds(n * part, part)], local_sem.at[n]
        )
        for n in range(parts)
    ]
    key_copies = [
        pltpu.make_async_copy(
            cache_hbm.at[k], keys.at[k, pl.ds(0, capacity)], local_sem.at[parts + k]
        )
        for k in range(holders)
    ]
    wv_copy = pltpu.make_async_copy(wv_hbm, wv, local_sem.at[parts + holders])
    for copy in wk_copies:
        copy.start()

    def at_column(e):
        return (rank, lax.rem(column + e + columns, columns))

    def at_group(d):
        return (lax.rem(rank + d + groups, groups), column)

    def remote(src, dst, send, recv, target):
        return pltpu.make_async_remote_copy(
            src_ref=src, dst_ref=dst, send_sem=send, recv_sem=recv,
            device_id=target, device_id_type=MESH,
        )

    barrier = pltpu.get_barrier_semaphore()
    for e in range(1, columns):
        pl.semaphore_signal(barrier, inc=1, device_id=at_column(e), device_id_type=MESH)
    for d in range(1, groups):
        pl.semaphore_signal(barrier, inc=1, device_id=at_group(d), device_id_type=MESH)

    def slot(e, k):
        return lax.rem(column + e, columns) * holders + k

    def turned(span, e, k):
        return jnp.concatenate(
            [rope_ref[span * PAIR + s, slot(e, k)] for s in range(PAIR)], axis=1
        )

    for k in range(movers):
        for e in range(columns):
            for s in range(PAIR):
                mine[k, s, e] = nope_ref[PAIR + s, slot(e, k)]
            mine[k, PAIR, e] = turned(1, e, k)
        shift_mine[k] = jnp.full(shift_mine.shape[1:], move_ref[0, k], jnp.int32)
        shift_of[0, k] = jnp.full(shift_mine.shape[1:], move_ref[0, k], jnp.int32)
    row = lax.broadcasted_iota(jnp.int32, (16, entries), 0)

    def fresh_rows(k):
        found = jnp.zeros((16, entries), jnp.float32)
        for j in range(steps):
            found = jnp.where(row == j, wide(fresh_ref[j])[k : k + 1], found)
        return found

    for k in range(holders):
        keys[k, pl.ds(capacity, EXTRA)] = jnp.zeros((EXTRA, entries), jnp.bfloat16)
        keys[k, pl.ds(capacity, 16)] = rounded(fresh_rows(k))
    for k in range(movers):
        mine_key[k] = rounded(fresh_rows(k))
    pl.semaphore_wait(barrier, columns - 1 + groups - 1)

    shift_copies = [
        remote(shift_mine, shift_of.at[e], shift_ss.at[e], shift_rs.at[e], at_column(-e))
        for e in range(1, columns)
    ]
    mine_copies = [
        remote(mine, moved.at[d - 1], mine_ss.at[d - 1], mine_rs.at[d - 1], at_group(-d))
        for d in range(1, groups)
    ]
    newer_copies = [
        remote(mine_key, moved_key.at[d - 1], key_ss.at[d - 1], key_rs.at[d - 1], at_group(-d))
        for d in range(1, groups)
    ]
    for copy in shift_copies + mine_copies + newer_copies:
        copy.start()
    for copy in key_copies:
        copy.start()
    wv_copy.start()

    def lat_copy(u, e):
        return remote(
            lat_send.at[u, e], lat_recv.at[u, e], lat_ss.at[u, e], lat_rs.at[u, e], at_column(e)
        )

    def rot_copy(u, e):
        return remote(
            rot_send.at[u, e], rot_recv.at[u, e], rot_ss.at[u, e], rot_rs.at[u, e], at_column(e)
        )

    def back_copy(u, e):
        return remote(
            back_send.at[u, e], back_recv.at[u, e], back_ss.at[u, e], back_rs.at[u, e],
            at_column(-e),
        )

    def chosen(e, k, options):
        found = wide(options(0))
        for d in range(2, groups):
            is_it = shift_of[e, k, 0:1, 0:1] == d
            found = jnp.where(is_it, wide(options(d - 1)), found)
        return found

    count = holders * columns * PAIR
    unit_rows = columns * PAIR * heads

    def place(k, e, s):
        return ((k * columns + e) * PAIR + s) * heads

    def absorb(span, first):
        for k in range(holders):
            for e in range(columns):
                for s in range(PAIR):
                    if span and k < movers:
                        value = chosen(e, k, lambda n: moved[n, k, s, e])
                    else:
                        value = wide(nope_ref[span * PAIR + s, slot(e, k)])
                    rows_in[pl.ds(place(k, e, s), heads)] = value
                if span and k < movers:
                    pair = rounded(chosen(e, k, lambda n: moved[n, k, PAIR, e]))
                else:
                    pair = turned(span, e, k)
                if e:
                    rot_send[span * holders + k, e] = pair
                else:
                    rot_recv[span * holders + k, 0] = pair
        for n in range(parts):
            if first:
                wk_copies[n].wait()

            def head(i, carry):
                picked = rounded(rows_in[pl.ds(i, count, stride=heads)])
                result = jnp.dot(picked, wk[i], preferred_element_type=jnp.float32)
                for c in range(latent // LANES):
                    rows_mid[c, pl.ds(i, count, stride=heads)] = result[:, lane(c)]
                return carry

            lax.fori_loop(n * part, (n + 1) * part, head, 0)
        for k in range(holders):
            u = span * holders + k
            for e in range(columns):
                at = pl.ds(place(k, e, 0), PAIR * heads)
                value = jnp.concatenate(
                    [rounded(rows_mid[c, at]) for c in range(latent // LANES)], axis=1
                )
                if e:
                    lat_send[u, e] = value
                    lat_copy(u, e).start()
                    rot_copy(u, e).start()
                else:
                    lat_recv[u, 0] = value

    absorb(0, True)
    for copy in shift_copies:
        copy.wait()
    for copy in mine_copies + newer_copies:
        copy.wait()
    for span in range(1, spans):
        absorb(span, False)
    for copy in key_copies:
        copy.wait()
    for k in range(movers):
        later = chosen(0, k, lambda n: moved_key[n, k])
        keys[k, pl.ds(capacity, 16)] = rounded(
            jnp.where(row < PAIR, wide(keys[k, pl.ds(capacity, 16)]), later)
        )

    at_key = lax.broadcasted_iota(jnp.int32, (1, total), 1)
    at_row = lax.broadcasted_iota(jnp.int32, (unit_rows, 1), 0)
    within = lax.rem(lax.div(at_row, heads), PAIR)

    def unit(u, carry):
        span = lax.div(u, holders)
        k = lax.rem(u, holders)
        for e in range(1, columns):
            lat_copy(u, e).wait_recv()
            rot_copy(u, e).wait_recv()
        live = length_ref[(rank * columns + column) * holders + k]
        token = jnp.where(at_key < capacity, steps, at_key - capacity)
        token = jnp.where(at_key < live, -1, token)
        nt = (((1,), (1,)), ((), ()))
        queries = lat_recv[u].reshape(unit_rows, latent)
        turns = rot_recv[u]
        turns = jnp.concatenate(
            [turns[e][:, s * rope : (s + 1) * rope] for e in range(columns) for s in range(PAIR)],
            axis=0,
        )
        scores = lax.dot_general(
            queries, keys[k, :, :latent], nt, preferred_element_type=jnp.float32
        ) + lax.dot_general(
            turns, keys[k, :, latent:], nt, preferred_element_type=jnp.float32
        )
        scores = jnp.where(token <= span * PAIR + within, scores * scale, -jnp.inf)
        spread = jnp.exp(scores - jnp.max(scores, axis=1, keepdims=True))
        weights = rounded(spread / jnp.sum(spread, axis=1, keepdims=True))
        mixed = rounded(
            jnp.dot(weights, keys[k, :, :latent], preferred_element_type=jnp.float32)
        ).reshape(columns, PAIR * heads, latent)
        back_recv[u, 0] = mixed[0]
        for e in range(1, columns):
            back_send[u, e] = mixed[e]
            back_copy(u, e).start()
        return carry

    lax.fori_loop(0, spans * holders, unit, 0)
    wv_copy.wait()

    def project(span, members):
        held = len(members)
        for n, k in enumerate(members):
            u = span * holders + k
            for e in range(1, columns):
                back_copy(u, e).wait_recv()
            for e in range(columns):
                value = wide(back_recv[u, e])
                for c in range(latent // LANES):
                    rows_mid[c, pl.ds(place(n, e, 0), PAIR * heads)] = value[:, lane(c)]

        def head(i, carry):
            at = pl.ds(i, held * columns * PAIR, stride=heads)
            picked = jnp.concatenate(
                [rounded(rows_mid[c, at]) for c in range(latent // LANES)], axis=1
            )
            rows_out[pl.ds(i, held * columns * PAIR, stride=heads)] = jnp.dot(
                picked, wv[i], preferred_element_type=jnp.float32
            )
            return carry

        lax.fori_loop(0, heads, head, 0)
        for n, k in enumerate(members):
            for e in range(columns):
                for s in range(PAIR):
                    value = rounded(rows_out[pl.ds(place(n, e, s), heads)])
                    if span and k < movers:
                        home[k, s, e] = value
                    else:
                        out_ref[span * PAIR + s, slot(e, k)] = value

    home_copies = [
        remote(home, home_recv.at[d - 1], home_ss.at[d - 1], home_rs.at[d - 1], at_group(d))
        for d in range(1, groups)
    ]
    project(0, list(range(holders)))
    project(1, list(range(movers)))
    for copy in home_copies:
        copy.start()
    if movers < holders:
        project(1, list(range(movers, holders)))
    for copy in home_copies:
        copy.wait()
    for k in range(movers):
        for e in range(columns):
            for s in range(PAIR):
                out_ref[PAIR + s, slot(e, k)] = rounded(
                    chosen(e, k, lambda n: home_recv[n, k, s, e])
                )

    def drain(u, carry):
        for e in range(1, columns):
            lat_copy(u, e).wait_send()
            rot_copy(u, e).wait_send()
            back_copy(u, e).wait_send()
        return carry

    lax.fori_loop(0, spans * holders, drain, 0)


def local_part(heads):
    return max(heads // 4, 1)


def body(q_nope, q_rope, w_absorb_k, w_absorb_v, latent_cache, new_latent, lengths, moves):
    steps, slots, heads, width = q_nope.shape
    rope = q_rope.shape[3]
    latent = w_absorb_k.shape[2]
    holders, capacity, entries = latent_cache.shape
    movers = moves.shape[1]
    groups = lax.axis_size("grp")
    columns = lax.axis_size("head")
    scale = YARN_GAIN / math.sqrt(width + rope)
    units = steps // PAIR * holders
    rows = holders * columns * PAIR * heads
    others = groups - 1
    bf16, f32 = jnp.bfloat16, jnp.float32
    dma = pltpu.SemaphoreType.DMA
    vmem = pl.BlockSpec(memory_space=pltpu.VMEM)
    smem = pl.BlockSpec(memory_space=pltpu.SMEM)
    hbm = pl.BlockSpec(memory_space=pl.ANY)
    parts = heads // local_part(heads)
    return pl.pallas_call(
        functools.partial(kernel, groups, columns, scale),
        out_shape=jax.ShapeDtypeStruct(q_nope.shape, bf16),
        in_specs=[smem, smem, vmem, vmem, vmem, hbm, hbm, hbm],
        out_specs=vmem,
        scratch_shapes=[
            pltpu.VMEM(w_absorb_k.shape, bf16),
            pltpu.VMEM(w_absorb_v.shape, bf16),
            pltpu.VMEM((holders, capacity + EXTRA, entries), bf16),
            dma((parts + holders + 1,)),
            pltpu.VMEM((rows, width), f32),
            pltpu.VMEM((latent // LANES, rows, LANES), f32),
            pltpu.VMEM((rows, width), f32),
            pltpu.VMEM((units, columns, PAIR * heads, latent), bf16),
            pltpu.VMEM((units, columns, PAIR * heads, latent), bf16),
            pltpu.VMEM((units, columns, heads, PAIR * rope), bf16),
            pltpu.VMEM((units, columns, heads, PAIR * rope), bf16),
            pltpu.VMEM((units, columns, PAIR * heads, latent), bf16),
            pltpu.VMEM((units, columns, PAIR * heads, latent), bf16),
            pltpu.VMEM((movers, PAIR + 1, columns, heads, width), bf16),
            pltpu.VMEM((others, movers, PAIR + 1, columns, heads, width), bf16),
            pltpu.VMEM((movers, 16, entries), bf16),
            pltpu.VMEM((others, movers, 16, entries), bf16),
            pltpu.VMEM((movers, PAIR, columns, heads, width), bf16),
            pltpu.VMEM((others, movers, PAIR, columns, heads, width), bf16),
            pltpu.VMEM((columns, movers, 8, LANES), jnp.int32),
            pltpu.VMEM((movers, 8, LANES), jnp.int32),
            dma((units, columns)), dma((units, columns)),
            dma((units, columns)), dma((units, columns)),
            dma((units, columns)), dma((units, columns)),
            dma((others,)), dma((others,)),
            dma((others,)), dma((others,)),
            dma((others,)), dma((others,)),
            dma((columns,)), dma((columns,)),
        ],
        compiler_params=pltpu.CompilerParams(
            collective_id=0, has_side_effects=True, vmem_limit_bytes=48 << 20
        ),
    )(lengths, moves, q_nope, q_rope, new_latent, w_absorb_k, w_absorb_v, latent_cache)


def solution(mesh):
    placed = (
        P(None, "grp", "head", None),
        P(None, "grp", "head", None),
        P("head", None, None),
        P("head", None, None),
        P(("grp", "head"), None, None),
        P(None, ("grp", "head"), None),
        P(),
        P("head", None),
    )
    return jax.shard_map(
        body, mesh=mesh, in_specs=placed, out_specs=P(None, "grp", "head", None), check_vma=False
    )
```

```python
import functools
import math

import jax
import jax.numpy as jnp
from jax import lax
from jax.experimental import pallas as pl
from jax.experimental.pallas import tpu as pltpu
from jax.sharding import PartitionSpec as P

PAIR = 2
EXTRA = 128
LANES = 128
YARN_GAIN = (0.1 * math.log(40.0) + 1.0) ** 2
MESH = pl.DeviceIdType.MESH


def lane(c):
    return slice(c * LANES, (c + 1) * LANES)


def rounded(value):
    return value.astype(jnp.bfloat16)


def wide(value):
    return value.astype(jnp.float32)


def kernel(
    groups, columns, scale,
    length_ref, move_ref, nope_ref, rope_ref, fresh_ref, wk_hbm, wv_hbm, cache_hbm,
    out_ref,
    wk, wv, keys, newer, local_sem,
    rows_in, rows_mid, rows_out,
    lat_send, lat_recv, rot_send, rot_recv, back_send, back_recv,
    mine, moved, mine_key, moved_key, home, home_recv, shift_of, shift_mine,
    lat_ss, lat_rs, rot_ss, rot_rs, back_ss, back_rs,
    mine_ss, mine_rs, key_ss, key_rs, home_ss, home_rs, shift_ss, shift_rs,
):
    steps, _, heads, _ = nope_ref.shape
    holders, entries, capacity = cache_hbm.shape
    latent = wk.shape[2]
    rope = entries - latent
    movers = move_ref.shape[1]
    spans = steps // PAIR
    total = capacity + EXTRA
    cuts = lat_send.shape[2]
    cut = heads // cuts
    rank = lax.axis_index("grp")
    column = lax.axis_index("head")
    parts = wk.shape[0] // local_part(heads)
    part = local_part(heads)

    wk_copies = [
        pltpu.make_async_copy(
            wk_hbm.at[pl.ds(n * part, part)], wk.at[pl.ds(n * part, part)], local_sem.at[n]
        )
        for n in range(parts)
    ]
    key_copies = [
        pltpu.make_async_copy(
            cache_hbm.at[k], keys.at[k], local_sem.at[parts + k]
        )
        for k in range(holders)
    ]
    wv_copy = pltpu.make_async_copy(wv_hbm, wv, local_sem.at[parts + holders])
    for copy in wk_copies:
        copy.start()

    def at_column(e):
        return (rank, lax.rem(column + e + columns, columns))

    def at_group(d):
        return (lax.rem(rank + d + groups, groups), column)

    def remote(src, dst, send, recv, target):
        return pltpu.make_async_remote_copy(
            src_ref=src, dst_ref=dst, send_sem=send, recv_sem=recv,
            device_id=target, device_id_type=MESH,
        )

    barrier = pltpu.get_barrier_semaphore()
    for e in range(1, columns):
        pl.semaphore_signal(barrier, inc=1, device_id=at_column(e), device_id_type=MESH)
    for d in range(1, groups):
        pl.semaphore_signal(barrier, inc=1, device_id=at_group(d), device_id_type=MESH)

    def slot(e, k):
        return lax.rem(column + e, columns) * holders + k

    def turned(span, e, k):
        return jnp.concatenate(
            [rope_ref[span * PAIR + s, slot(e, k)] for s in range(PAIR)], axis=1
        )

    for k in range(movers):
        for e in range(columns):
            for s in range(PAIR):
                mine[k, s, e] = nope_ref[PAIR + s, slot(e, k)]
            mine[k, PAIR, e] = turned(1, e, k)
        shift_mine[k] = jnp.full(shift_mine.shape[1:], move_ref[0, k], jnp.int32)
        shift_of[0, k] = jnp.full(shift_mine.shape[1:], move_ref[0, k], jnp.int32)
    row = lax.broadcasted_iota(jnp.int32, (16, entries), 0)

    def fresh_rows(k):
        found = jnp.zeros((16, entries), jnp.float32)
        for j in range(steps):
            found = jnp.where(row == j, wide(fresh_ref[j])[k : k + 1], found)
        return found

    for k in range(holders):
        newer[k] = jnp.zeros((EXTRA, entries), jnp.bfloat16)
        newer[k, 0:16] = rounded(fresh_rows(k))
    for k in range(movers):
        mine_key[k] = rounded(fresh_rows(k))
    pl.semaphore_wait(barrier, columns - 1 + groups - 1)

    shift_copies = [
        remote(shift_mine, shift_of.at[e], shift_ss.at[e], shift_rs.at[e], at_column(-e))
        for e in range(1, columns)
    ]
    mine_copies = [
        remote(mine, moved.at[d - 1], mine_ss.at[d - 1], mine_rs.at[d - 1], at_group(-d))
        for d in range(1, groups)
    ]
    newer_copies = [
        remote(mine_key, moved_key.at[d - 1], key_ss.at[d - 1], key_rs.at[d - 1], at_group(-d))
        for d in range(1, groups)
    ]
    for copy in shift_copies + mine_copies + newer_copies:
        copy.start()
    for copy in key_copies:
        copy.start()
    wv_copy.start()

    def lat_copy(u, e, c):
        return remote(
            lat_send.at[u, e, c], lat_recv.at[u, e, c], lat_ss.at[u, e, c], lat_rs.at[u, e, c],
            at_column(e),
        )

    def rot_copy(u, e):
        return remote(
            rot_send.at[u, e], rot_recv.at[u, e], rot_ss.at[u, e], rot_rs.at[u, e], at_column(e)
        )

    def back_copy(u, e):
        return remote(
            back_send.at[u, e], back_recv.at[u, e], back_ss.at[u, e], back_rs.at[u, e],
            at_column(-e),
        )

    low, high = jnp.int32(0), jnp.int32(columns - 1)
    upward, downward = [], []
    for _ in range(columns - 1):
        take_high = high - column >= column - low
        target = jnp.where(take_high, high, low)
        upward.append(lax.rem(target - column + columns, columns))
        downward.append(lax.rem(column - target + columns, columns))
        high = jnp.where(take_high, high - 1, high)
        low = jnp.where(take_high, low, low + 1)

    def chosen(e, k, options):
        found = wide(options(0))
        for d in range(2, groups):
            is_it = shift_of[e, k, 0:1, 0:1] == d
            found = jnp.where(is_it, wide(options(d - 1)), found)
        return found

    count = holders * columns * PAIR
    unit_rows = columns * PAIR * heads

    def place(k, e, s):
        return ((k * columns + e) * PAIR + s) * heads

    def turn(span, k):
        u = span * holders + k
        for e in range(columns):
            if span and k < movers:
                pair = rounded(chosen(e, k, lambda n: moved[n, k, PAIR, e]))
            else:
                pair = turned(span, e, k)
            if e:
                rot_send[u, e] = pair
            else:
                rot_recv[u, 0] = pair
        for e in upward:
            rot_copy(u, e).start()

    def absorb(span, first):
        for k in range(holders):
            for e in range(columns):
                for s in range(PAIR):
                    if span and k < movers:
                        value = chosen(e, k, lambda n: moved[n, k, s, e])
                    else:
                        value = wide(nope_ref[span * PAIR + s, slot(e, k)])
                    rows_in[pl.ds(place(k, e, s), heads)] = value
        for n in range(parts):
            if first:
                wk_copies[n].wait()

            def head(i, carry):
                picked = rounded(rows_in[pl.ds(i, count, stride=heads)])
                result = jnp.dot(picked, wk[i], preferred_element_type=jnp.float32)
                for c in range(latent // LANES):
                    rows_mid[c, pl.ds(i, count, stride=heads)] = result[:, lane(c)]
                return carry

            lax.fori_loop(n * part, (n + 1) * part, head, 0, unroll=True)
            if (n + 1) % (parts // cuts):
                continue
            c = n // (parts // cuts)
            for k in range(holders):
                u = span * holders + k
                for e in range(columns):
                    value = jnp.concatenate(
                        [
                            jnp.concatenate(
                                [
                                    rounded(rows_mid[l, pl.ds(place(k, e, s) + c * cut, cut)])
                                    for l in range(latent // LANES)
                                ],
                                axis=1,
                            )
                            for s in range(PAIR)
                        ],
                        axis=0,
                    )
                    if e:
                        lat_send[u, e, c] = value
                    else:
                        lat_recv[u, 0, c] = value
                for e in upward:
                    lat_copy(u, e, c).start()

    for k in range(holders):
        turn(0, k)
    for k in range(movers, holders):
        turn(1, k)
    absorb(0, True)
    for copy in shift_copies:
        copy.wait()
    for copy in mine_copies + newer_copies:
        copy.wait()
    for k in range(movers):
        turn(1, k)
    absorb(1, False)
    for copy in key_copies:
        copy.wait()
    for k in range(movers):
        later = chosen(0, k, lambda n: moved_key[n, k])
        newer[k, 0:16] = rounded(jnp.where(row < PAIR, wide(newer[k, 0:16]), later))

    at_key = lax.broadcasted_iota(jnp.int32, (1, total), 1)
    at_row = lax.broadcasted_iota(jnp.int32, (unit_rows, 1), 0)
    within = lax.rem(lax.div(at_row, cut), PAIR)

    def unit(u, carry):
        span = lax.div(u, holders)
        k = lax.rem(u, holders)
        for e in range(1, columns):
            for c in range(cuts):
                lat_copy(u, e, c).wait_recv()
            rot_copy(u, e).wait_recv()
        live = length_ref[(rank * columns + column) * holders + k]
        token = jnp.where(at_key < capacity, steps, at_key - capacity)
        token = jnp.where(at_key < live, -1, token)
        nt = (((1,), (1,)), ((), ()))
        queries = lat_recv[u].reshape(unit_rows, latent)
        turns = rot_recv[u]
        turns = jnp.concatenate(
            [
                turns[e][c * cut : (c + 1) * cut, s * rope : (s + 1) * rope]
                for e in range(columns)
                for c in range(cuts)
                for s in range(PAIR)
            ],
            axis=0,
        )
        cached = jnp.dot(
            queries, keys[k, :latent], preferred_element_type=jnp.float32
        ) + jnp.dot(turns, keys[k, latent:], preferred_element_type=jnp.float32)
        decoded = lax.dot_general(
            queries, newer[k, :, :latent], nt, preferred_element_type=jnp.float32
        ) + lax.dot_general(
            turns, newer[k, :, latent:], nt, preferred_element_type=jnp.float32
        )
        scores = jnp.concatenate([cached, decoded], axis=1)
        scores = jnp.where(token <= span * PAIR + within, scores * scale, -jnp.inf)
        spread = jnp.exp(scores - jnp.max(scores, axis=1, keepdims=True))
        weights = rounded(spread / jnp.sum(spread, axis=1, keepdims=True))
        mixed = rounded(
            lax.dot_general(
                weights[:, :capacity], keys[k, :latent], nt, preferred_element_type=jnp.float32
            )
            + jnp.dot(
                weights[:, capacity:], newer[k, :, :latent], preferred_element_type=jnp.float32
            )
        ).reshape(columns, PAIR * heads, latent)
        back_recv[u, 0] = mixed[0]
        for e in range(1, columns):
            back_send[u, e] = mixed[e]
        for e in downward:
            back_copy(u, e).start()
        return carry

    lax.fori_loop(0, spans * holders, unit, 0)
    wv_copy.wait()

    def project(span, members):
        held = len(members)
        for n, k in enumerate(members):
            u = span * holders + k
            for e in range(1, columns):
                back_copy(u, e).wait_recv()
            for e in range(columns):
                value = wide(back_recv[u, e])
                for c in range(cuts):
                    for s in range(PAIR):
                        at = (c * PAIR + s) * cut
                        for l in range(latent // LANES):
                            rows_mid[l, pl.ds(place(n, e, s) + c * cut, cut)] = value[
                                at : at + cut, lane(l)
                            ]

        def head(i, carry):
            at = pl.ds(i, held * columns * PAIR, stride=heads)
            picked = jnp.concatenate(
                [rounded(rows_mid[c, at]) for c in range(latent // LANES)], axis=1
            )
            rows_out[pl.ds(i, held * columns * PAIR, stride=heads)] = jnp.dot(
                picked, wv[i], preferred_element_type=jnp.float32
            )
            return carry

        lax.fori_loop(0, heads, head, 0, unroll=min(heads, 8))
        for n, k in enumerate(members):
            for e in range(columns):
                for s in range(PAIR):
                    value = rounded(rows_out[pl.ds(place(n, e, s), heads)])
                    if span and k < movers:
                        home[k, s, e] = value
                    else:
                        out_ref[span * PAIR + s, slot(e, k)] = value

    home_copies = [
        remote(home, home_recv.at[d - 1], home_ss.at[d - 1], home_rs.at[d - 1], at_group(d))
        for d in range(1, groups)
    ]
    project(0, list(range(holders)))
    project(1, list(range(movers)))
    for copy in home_copies:
        copy.start()
    if movers < holders:
        project(1, list(range(movers, holders)))
    for copy in home_copies:
        copy.wait()
    for k in range(movers):
        for e in range(columns):
            for s in range(PAIR):
                out_ref[PAIR + s, slot(e, k)] = rounded(
                    chosen(e, k, lambda n: home_recv[n, k, s, e])
                )

    def drain(u, carry):
        for e in range(1, columns):
            for c in range(cuts):
                lat_copy(u, e, c).wait_send()
            rot_copy(u, e).wait_send()
            back_copy(u, e).wait_send()
        return carry

    lax.fori_loop(0, spans * holders, drain, 0)


def local_part(heads):
    return max(heads // 4, 1)


def body(q_nope, q_rope, w_absorb_k, w_absorb_v, latent_cache, new_latent, lengths, moves):
    steps, slots, heads, width = q_nope.shape
    rope = q_rope.shape[3]
    latent = w_absorb_k.shape[2]
    holders, capacity, entries = latent_cache.shape
    movers = moves.shape[1]
    groups = lax.axis_size("grp")
    columns = lax.axis_size("head")
    scale = YARN_GAIN / math.sqrt(width + rope)
    assert steps == 2 * PAIR
    units = steps // PAIR * holders
    rows = holders * columns * PAIR * heads
    others = groups - 1
    bf16, f32 = jnp.bfloat16, jnp.float32
    dma = pltpu.SemaphoreType.DMA
    vmem = pl.BlockSpec(memory_space=pltpu.VMEM)
    smem = pl.BlockSpec(memory_space=pltpu.SMEM)
    hbm = pl.BlockSpec(memory_space=pl.ANY)
    parts = heads // local_part(heads)
    cuts = 1 if heads % 32 else 2
    return pl.pallas_call(
        functools.partial(kernel, groups, columns, scale),
        out_shape=jax.ShapeDtypeStruct(q_nope.shape, bf16),
        in_specs=[smem, smem, vmem, vmem, vmem, hbm, hbm, hbm],
        out_specs=vmem,
        scratch_shapes=[
            pltpu.VMEM(w_absorb_k.shape, bf16),
            pltpu.VMEM(w_absorb_v.shape, bf16),
            pltpu.VMEM((holders, entries, capacity), bf16),
            pltpu.VMEM((holders, EXTRA, entries), bf16),
            dma((parts + holders + 1,)),
            pltpu.VMEM((rows, width), f32),
            pltpu.VMEM((latent // LANES, rows, LANES), f32),
            pltpu.VMEM((rows, width), f32),
            pltpu.VMEM((units, columns, cuts, PAIR * heads // cuts, latent), bf16),
            pltpu.VMEM((units, columns, cuts, PAIR * heads // cuts, latent), bf16),
            pltpu.VMEM((units, columns, heads, PAIR * rope), bf16),
            pltpu.VMEM((units, columns, heads, PAIR * rope), bf16),
            pltpu.VMEM((units, columns, PAIR * heads, latent), bf16),
            pltpu.VMEM((units, columns, PAIR * heads, latent), bf16),
            pltpu.VMEM((movers, PAIR + 1, columns, heads, width), bf16),
            pltpu.VMEM((others, movers, PAIR + 1, columns, heads, width), bf16),
            pltpu.VMEM((movers, 16, entries), bf16),
            pltpu.VMEM((others, movers, 16, entries), bf16),
            pltpu.VMEM((movers, PAIR, columns, heads, width), bf16),
            pltpu.VMEM((others, movers, PAIR, columns, heads, width), bf16),
            pltpu.VMEM((columns, movers, 8, LANES), jnp.int32),
            pltpu.VMEM((movers, 8, LANES), jnp.int32),
            dma((units, columns, cuts)), dma((units, columns, cuts)),
            dma((units, columns)), dma((units, columns)),
            dma((units, columns)), dma((units, columns)),
            dma((others,)), dma((others,)),
            dma((others,)), dma((others,)),
            dma((others,)), dma((others,)),
            dma((columns,)), dma((columns,)),
        ],
        compiler_params=pltpu.CompilerParams(
            collective_id=0, has_side_effects=True, vmem_limit_bytes=48 << 20
        ),
    )(lengths, moves, q_nope, q_rope, new_latent, w_absorb_k, w_absorb_v, jnp.swapaxes(latent_cache, 1, 2))


def solution(mesh):
    placed = (
        P(None, "grp", "head", None),
        P(None, "grp", "head", None),
        P("head", None, None),
        P("head", None, None),
        P(("grp", "head"), None, None),
        P(None, ("grp", "head"), None),
        P(),
        P("head", None),
    )
    return jax.shard_map(
        body, mesh=mesh, in_specs=placed, out_specs=P(None, "grp", "head", None), check_vma=False
    )
```

```python
import functools
import math

import jax
import jax.numpy as jnp
from jax import lax
from jax.experimental import pallas as pl
from jax.experimental.pallas import tpu as pltpu
from jax.sharding import PartitionSpec as P

PAIR = 2
EXTRA = 128
LANES = 128
YARN_GAIN = (0.1 * math.log(40.0) + 1.0) ** 2
MESH = pl.DeviceIdType.MESH


def lane(c):
    return slice(c * LANES, (c + 1) * LANES)


def rounded(value):
    return value.astype(jnp.bfloat16)


def wide(value):
    return value.astype(jnp.float32)


def kernel(
    groups, columns, scale,
    length_ref, move_ref, nope_hbm, rope_hbm, fresh_hbm, wk_hbm, wv_hbm, cache_hbm,
    out_ref,
    nope_ref, rope_ref, fresh_ref, entry_sem,
    wk, wv, keys, newer, local_sem,
    rows_in, rows_mid, rows_out,
    lat_send, lat_recv, rot_send, rot_recv, back_send, back_recv,
    mine, moved, mine_key, moved_key, home, home_recv, shift_of, shift_mine,
    lat_ss, lat_rs, rot_ss, rot_rs, back_ss, back_rs,
    mine_ss, mine_rs, key_ss, key_rs, home_ss, home_rs, shift_ss, shift_rs,
):
    steps, _, heads, _ = nope_ref.shape
    holders, entries, capacity = cache_hbm.shape
    latent = wk.shape[2]
    rope = entries - latent
    movers = move_ref.shape[1]
    spans = steps // PAIR
    total = capacity + EXTRA
    cuts = lat_send.shape[2]
    cut = heads // cuts
    rank = lax.axis_index("grp")
    column = lax.axis_index("head")
    parts = wk.shape[0] // local_part(heads)
    part = local_part(heads)

    wk_copies = [
        pltpu.make_async_copy(
            wk_hbm.at[pl.ds(n * part, part)], wk.at[pl.ds(n * part, part)], local_sem.at[n]
        )
        for n in range(parts)
    ]
    key_copies = [
        pltpu.make_async_copy(
            cache_hbm.at[k], keys.at[k], local_sem.at[parts + k]
        )
        for k in range(holders)
    ]
    wv_copy = pltpu.make_async_copy(wv_hbm, wv, local_sem.at[parts + holders])
    entry_copies = [
        pltpu.make_async_copy(src, dst, entry_sem.at[n])
        for n, (src, dst) in enumerate(
            ((rope_hbm, rope_ref), (nope_hbm, nope_ref), (fresh_hbm, fresh_ref))
        )
    ]
    for copy in entry_copies + wk_copies:
        copy.start()

    def at_column(e):
        return (rank, lax.rem(column + e + columns, columns))

    def at_group(d):
        return (lax.rem(rank + d + groups, groups), column)

    def remote(src, dst, send, recv, target):
        return pltpu.make_async_remote_copy(
            src_ref=src, dst_ref=dst, send_sem=send, recv_sem=recv,
            device_id=target, device_id_type=MESH,
        )

    barrier = pltpu.get_barrier_semaphore()
    for e in range(1, columns):
        pl.semaphore_signal(barrier, inc=1, device_id=at_column(e), device_id_type=MESH)
    for d in range(1, groups):
        pl.semaphore_signal(barrier, inc=1, device_id=at_group(d), device_id_type=MESH)

    def slot(e, k):
        return lax.rem(column + e, columns) * holders + k

    def turned(span, e, k):
        return jnp.concatenate(
            [rope_ref[span * PAIR + s, slot(e, k)] for s in range(PAIR)], axis=1
        )

    for copy in entry_copies:
        copy.wait()
    for k in range(movers):
        for e in range(columns):
            for s in range(PAIR):
                mine[k, s, e] = nope_ref[PAIR + s, slot(e, k)]
            mine[k, PAIR, e] = turned(1, e, k)
        shift_mine[k] = jnp.full(shift_mine.shape[1:], move_ref[0, k], jnp.int32)
        shift_of[0, k] = jnp.full(shift_mine.shape[1:], move_ref[0, k], jnp.int32)
    row = lax.broadcasted_iota(jnp.int32, (16, entries), 0)

    def fresh_rows(k):
        found = jnp.zeros((16, entries), jnp.float32)
        for j in range(steps):
            found = jnp.where(row == j, wide(fresh_ref[j])[k : k + 1], found)
        return found

    for k in range(holders):
        newer[k] = jnp.zeros((EXTRA, entries), jnp.bfloat16)
        newer[k, 0:16] = rounded(fresh_rows(k))
    for k in range(movers):
        mine_key[k] = rounded(fresh_rows(k))
    pl.semaphore_wait(barrier, columns - 1 + groups - 1)

    shift_copies = [
        remote(shift_mine, shift_of.at[e], shift_ss.at[e], shift_rs.at[e], at_column(-e))
        for e in range(1, columns)
    ]
    mine_copies = [
        remote(mine, moved.at[d - 1], mine_ss.at[d - 1], mine_rs.at[d - 1], at_group(-d))
        for d in range(1, groups)
    ]
    newer_copies = [
        remote(mine_key, moved_key.at[d - 1], key_ss.at[d - 1], key_rs.at[d - 1], at_group(-d))
        for d in range(1, groups)
    ]
    for copy in shift_copies + mine_copies + newer_copies:
        copy.start()

    def lat_copy(u, e, c):
        return remote(
            lat_send.at[u, e, c], lat_recv.at[u, e, c], lat_ss.at[u, e, c], lat_rs.at[u, e, c],
            at_column(e),
        )

    def rot_copy(u, e):
        return remote(
            rot_send.at[u, e], rot_recv.at[u, e], rot_ss.at[u, e], rot_rs.at[u, e], at_column(e)
        )

    def back_copy(u, e):
        return remote(
            back_send.at[u, e], back_recv.at[u, e], back_ss.at[u, e], back_rs.at[u, e],
            at_column(-e),
        )

    low, high = jnp.int32(0), jnp.int32(columns - 1)
    upward, downward = [], []
    for _ in range(columns - 1):
        take_high = high - column >= column - low
        target = jnp.where(take_high, high, low)
        upward.append(lax.rem(target - column + columns, columns))
        downward.append(lax.rem(column - target + columns, columns))
        high = jnp.where(take_high, high - 1, high)
        low = jnp.where(take_high, low, low + 1)

    def chosen(e, k, options):
        found = wide(options(0))
        for d in range(2, groups):
            is_it = shift_of[e, k, 0:1, 0:1] == d
            found = jnp.where(is_it, wide(options(d - 1)), found)
        return found

    unit_rows = columns * PAIR * heads

    def place(k, e, s):
        return ((k * columns + e) * PAIR + s) * heads

    def turn(span, k):
        u = span * holders + k
        for e in range(columns):
            if span and k < movers:
                pair = rounded(chosen(e, k, lambda n: moved[n, k, PAIR, e]))
            else:
                pair = turned(span, e, k)
            if e:
                rot_send[u, e] = pair
            else:
                rot_recv[u, 0] = pair
        for e in upward:
            rot_copy(u, e).start()

    def absorb(members, first):
        count = len(members) * columns * PAIR
        for m, (span, k) in enumerate(members):
            for e in range(columns):
                for s in range(PAIR):
                    if span and k < movers:
                        value = chosen(e, k, lambda n: moved[n, k, s, e])
                    else:
                        value = wide(nope_ref[span * PAIR + s, slot(e, k)])
                    rows_in[pl.ds(place(m, e, s), heads)] = value
        for n in range(parts):
            if first:
                wk_copies[n].wait()

            def head(i, carry):
                picked = rounded(rows_in[pl.ds(i, count, stride=heads)])
                result = jnp.dot(picked, wk[i], preferred_element_type=jnp.float32)
                for c in range(latent // LANES):
                    rows_mid[c, pl.ds(i, count, stride=heads)] = result[:, lane(c)]
                return carry

            lax.fori_loop(n * part, (n + 1) * part, head, 0, unroll=True)
            if (n + 1) % (parts // cuts):
                continue
            c = n // (parts // cuts)
            for m, (span, k) in enumerate(members):
                u = span * holders + k
                for e in range(columns):
                    value = jnp.concatenate(
                        [
                            jnp.concatenate(
                                [
                                    rounded(rows_mid[l, pl.ds(place(m, e, s) + c * cut, cut)])
                                    for l in range(latent // LANES)
                                ],
                                axis=1,
                            )
                            for s in range(PAIR)
                        ],
                        axis=0,
                    )
                    if e:
                        lat_send[u, e, c] = value
                    else:
                        lat_recv[u, 0, c] = value
                for e in upward:
                    lat_copy(u, e, c).start()

    settled = [(0, k) for k in range(holders)] + [(1, k) for k in range(movers, holders)]
    moving = [(1, k) for k in range(movers)]
    for span, k in settled:
        turn(span, k)
    absorb(settled, True)
    for copy in key_copies:
        copy.start()
    for copy in shift_copies:
        copy.wait()
    for copy in mine_copies + newer_copies:
        copy.wait()
    for span, k in moving:
        turn(span, k)
    absorb(moving, False)
    wv_copy.start()
    for copy in key_copies:
        copy.wait()
    for k in range(movers):
        later = chosen(0, k, lambda n: moved_key[n, k])
        newer[k, 0:16] = rounded(jnp.where(row < PAIR, wide(newer[k, 0:16]), later))

    at_key = lax.broadcasted_iota(jnp.int32, (1, total), 1)
    at_row = lax.broadcasted_iota(jnp.int32, (unit_rows, 1), 0)
    within = lax.rem(lax.div(at_row, cut), PAIR)

    def unit(u, carry):
        span = lax.div(u, holders)
        k = lax.rem(u, holders)
        for e in range(1, columns):
            for c in range(cuts):
                lat_copy(u, e, c).wait_recv()
            rot_copy(u, e).wait_recv()
        live = length_ref[(rank * columns + column) * holders + k]
        token = jnp.where(at_key < capacity, steps, at_key - capacity)
        token = jnp.where(at_key < live, -1, token)
        nt = (((1,), (1,)), ((), ()))
        queries = lat_recv[u].reshape(unit_rows, latent)
        turns = rot_recv[u]
        turns = jnp.concatenate(
            [
                turns[e][c * cut : (c + 1) * cut, s * rope : (s + 1) * rope]
                for e in range(columns)
                for c in range(cuts)
                for s in range(PAIR)
            ],
            axis=0,
        )
        cached = jnp.dot(
            queries, keys[k, :latent], preferred_element_type=jnp.float32
        ) + jnp.dot(turns, keys[k, latent:], preferred_element_type=jnp.float32)
        decoded = lax.dot_general(
            queries, newer[k, :, :latent], nt, preferred_element_type=jnp.float32
        ) + lax.dot_general(
            turns, newer[k, :, latent:], nt, preferred_element_type=jnp.float32
        )
        scores = jnp.concatenate([cached, decoded], axis=1)
        scores = jnp.where(token <= span * PAIR + within, scores * scale, -jnp.inf)
        spread = jnp.exp(scores - jnp.max(scores, axis=1, keepdims=True))
        weights = rounded(spread / jnp.sum(spread, axis=1, keepdims=True))
        mixed = rounded(
            lax.dot_general(
                weights[:, :capacity], keys[k, :latent], nt, preferred_element_type=jnp.float32
            )
            + jnp.dot(
                weights[:, capacity:], newer[k, :, :latent], preferred_element_type=jnp.float32
            )
        ).reshape(columns, PAIR * heads, latent)
        back_recv[u, 0] = mixed[0]
        for e in range(1, columns):
            back_send[u, e] = mixed[e]
        for e in downward:
            back_copy(u, e).start()
        return carry

    lax.fori_loop(0, spans * holders, unit, 0)
    wv_copy.wait()

    def project(span, members):
        held = len(members)
        for n, k in enumerate(members):
            u = span * holders + k
            for e in range(1, columns):
                back_copy(u, e).wait_recv()
            for e in range(columns):
                value = wide(back_recv[u, e])
                for c in range(cuts):
                    for s in range(PAIR):
                        at = (c * PAIR + s) * cut
                        for l in range(latent // LANES):
                            rows_mid[l, pl.ds(place(n, e, s) + c * cut, cut)] = value[
                                at : at + cut, lane(l)
                            ]

        def head(i, carry):
            at = pl.ds(i, held * columns * PAIR, stride=heads)
            picked = jnp.concatenate(
                [rounded(rows_mid[c, at]) for c in range(latent // LANES)], axis=1
            )
            rows_out[pl.ds(i, held * columns * PAIR, stride=heads)] = jnp.dot(
                picked, wv[i], preferred_element_type=jnp.float32
            )
            return carry

        lax.fori_loop(0, heads, head, 0, unroll=min(heads, 8))
        for n, k in enumerate(members):
            for e in range(columns):
                for s in range(PAIR):
                    value = rounded(rows_out[pl.ds(place(n, e, s), heads)])
                    if span and k < movers:
                        home[k, s, e] = value
                    else:
                        out_ref[span * PAIR + s, slot(e, k)] = value

    home_copies = [
        remote(home, home_recv.at[d - 1], home_ss.at[d - 1], home_rs.at[d - 1], at_group(d))
        for d in range(1, groups)
    ]
    project(0, list(range(holders)))
    project(1, list(range(movers)))
    for copy in home_copies:
        copy.start()
    if movers < holders:
        project(1, list(range(movers, holders)))
    for copy in home_copies:
        copy.wait()
    for k in range(movers):
        for e in range(columns):
            for s in range(PAIR):
                out_ref[PAIR + s, slot(e, k)] = rounded(
                    chosen(e, k, lambda n: home_recv[n, k, s, e])
                )

    def drain(u, carry):
        for e in range(1, columns):
            for c in range(cuts):
                lat_copy(u, e, c).wait_send()
            rot_copy(u, e).wait_send()
            back_copy(u, e).wait_send()
        return carry

    lax.fori_loop(0, spans * holders, drain, 0)


def local_part(heads):
    return max(heads // 4, 1)


def body(q_nope, q_rope, w_absorb_k, w_absorb_v, latent_cache, new_latent, lengths, moves):
    steps, slots, heads, width = q_nope.shape
    rope = q_rope.shape[3]
    latent = w_absorb_k.shape[2]
    holders, capacity, entries = latent_cache.shape
    movers = moves.shape[1]
    groups = lax.axis_size("grp")
    columns = lax.axis_size("head")
    scale = YARN_GAIN / math.sqrt(width + rope)
    assert steps == 2 * PAIR
    units = steps // PAIR * holders
    rows = (2 * holders - movers) * columns * PAIR * heads
    others = groups - 1
    bf16, f32 = jnp.bfloat16, jnp.float32
    dma = pltpu.SemaphoreType.DMA
    vmem = pl.BlockSpec(memory_space=pltpu.VMEM)
    smem = pl.BlockSpec(memory_space=pltpu.SMEM)
    hbm = pl.BlockSpec(memory_space=pl.ANY)
    parts = heads // local_part(heads)
    cuts = 1 if heads % 32 else 2
    return pl.pallas_call(
        functools.partial(kernel, groups, columns, scale),
        out_shape=jax.ShapeDtypeStruct(q_nope.shape, bf16),
        in_specs=[smem, smem, hbm, hbm, hbm, hbm, hbm, hbm],
        out_specs=vmem,
        scratch_shapes=[
            pltpu.VMEM(q_nope.shape, bf16),
            pltpu.VMEM(q_rope.shape, bf16),
            pltpu.VMEM(new_latent.shape, bf16),
            dma((3,)),
            pltpu.VMEM(w_absorb_k.shape, bf16),
            pltpu.VMEM(w_absorb_v.shape, bf16),
            pltpu.VMEM((holders, entries, capacity), bf16),
            pltpu.VMEM((holders, EXTRA, entries), bf16),
            dma((parts + holders + 1,)),
            pltpu.VMEM((rows, width), f32),
            pltpu.VMEM((latent // LANES, rows, LANES), f32),
            pltpu.VMEM((rows, width), f32),
            pltpu.VMEM((units, columns, cuts, PAIR * heads // cuts, latent), bf16),
            pltpu.VMEM((units, columns, cuts, PAIR * heads // cuts, latent), bf16),
            pltpu.VMEM((units, columns, heads, PAIR * rope), bf16),
            pltpu.VMEM((units, columns, heads, PAIR * rope), bf16),
            pltpu.VMEM((units, columns, PAIR * heads, latent), bf16),
            pltpu.VMEM((units, columns, PAIR * heads, latent), bf16),
            pltpu.VMEM((movers, PAIR + 1, columns, heads, width), bf16),
            pltpu.VMEM((others, movers, PAIR + 1, columns, heads, width), bf16),
            pltpu.VMEM((movers, 16, entries), bf16),
            pltpu.VMEM((others, movers, 16, entries), bf16),
            pltpu.VMEM((movers, PAIR, columns, heads, width), bf16),
            pltpu.VMEM((others, movers, PAIR, columns, heads, width), bf16),
            pltpu.VMEM((columns, movers, 8, LANES), jnp.int32),
            pltpu.VMEM((movers, 8, LANES), jnp.int32),
            dma((units, columns, cuts)), dma((units, columns, cuts)),
            dma((units, columns)), dma((units, columns)),
            dma((units, columns)), dma((units, columns)),
            dma((others,)), dma((others,)),
            dma((others,)), dma((others,)),
            dma((others,)), dma((others,)),
            dma((columns,)), dma((columns,)),
        ],
        compiler_params=pltpu.CompilerParams(
            collective_id=0, has_side_effects=True, vmem_limit_bytes=60 << 20
        ),
    )(lengths, moves, q_nope, q_rope, new_latent, w_absorb_k, w_absorb_v, jnp.swapaxes(latent_cache, 1, 2))


def solution(mesh):
    placed = (
        P(None, "grp", "head", None),
        P(None, "grp", "head", None),
        P("head", None, None),
        P("head", None, None),
        P(("grp", "head"), None, None),
        P(None, ("grp", "head"), None),
        P(),
        P("head", None),
    )
    return jax.shard_map(
        body, mesh=mesh, in_specs=placed, out_specs=P(None, "grp", "head", None), check_vma=False
    )
```
